32 devices in a mesh: groups: 2 (over y), arc: 4 (over z), sec: 2 (over x), rep: 2 (over core).
Axes of the slice: x: 2, y: 2, z: 4, core: 2. Of those that a mesh axis runs over, the one named last changes fastest.
Arguments:
- slip_state: float32 [4096, 256], P(('groups', 'arc', 'sec', 'rep')), parts along dimension 0, may hold values from -6 to 6
- strain: float32 [6, 4096], P(None, ('groups', 'arc', 'sec', 'rep')), parts along dimension 1, may hold values from -6 to 6
- counts: int32 [4096], P(('groups', 'arc', 'sec', 'rep')), parts along dimension 0, may hold values from 1 to 12, as said below
- element_stiffness: float32 [6, 6, 4096], P(None, None, ('groups', 'arc', 'sec', 'rep')), parts along dimension 2, as said below
- foundation: float32 [6, 4096], P(None, ('groups', 'arc', 'sec', 'rep')), parts along dimension 1, may hold values from 0.01 to 0.1
- external_load: float32 [6, 4096], P(None, ('groups', 'arc', 'sec', 'rep')), parts along dimension 1, may hold values from -6 to 6
- stiffness_micro: float32 [256, 256], replicated, as said below
- tangent_inverse: float32 [256, 256], replicated
- friction_limit: float32 [256], replicated, may hold values from 0.2 to 2
- slip_scale: float32 [256], replicated, may hold values from 0.3 to 3
- section_map: float32 [6, 256], replicated, may hold values from -2.5 to 2.5
Outputs:
- new_slip: float32 [4096, 256], P(('groups', 'arc', 'sec', 'rep')), parts along dimension 0
- increment: float32 [6, 4096], P(None, ('groups', 'arc', 'sec', 'rep')), parts along dimension 1
The draws below stay inside these ranges and needn't reach their ends.
There are 2 independent parts, one for each index of `groups`. The reference program is written for one: setup_inputs(seed, part) draws one part's arguments, and reference() takes and returns one part's arrays. A program takes and returns all parts, laid end to end along the dimension named above; an argument that names none is the same for every part. Nothing has to cross between parts.
Inputs may be any that keep to these rules, and one draw needn't show every extreme that they name: counts[p] is the number of slip sweeps of node p in each Newton iteration. Every element_stiffness[:, :, i] is symmetric and each diagonal entry exceeds the sum of the magnitudes of the other entries of its row. stiffness_micro is symmetric and each diagonal entry exceeds the sum of the magnitudes of the other entries of its row.
All inputs are finite; a program needn't handle non-finite values.
Results may differ from the reference program's by a relative error of at most 0.00055.
Values sent between devices are 32-bit elements; how exact they have to be, the bound alone decides.
A program may use at most 64 MiB of HBM per device.

```python
import math
import jax
import jax.numpy as jnp
from jax import lax

NS = 256
BLOCK = 6
NEWTON = 2
MAXC = 12
POINTS = 2048


stiff_scale = 300.0


def draw_counts(key, part):
    node_index = jnp.arange(POINTS, dtype=jnp.int32)
    bucket_index = node_index * 64 // POINTS
    ramp = 10 * bucket_index * bucket_index // 4096
    extra = jax.random.randint(key, (POINTS,), 0, 3, dtype=jnp.int32)
    result = jnp.minimum(MAXC, 1 + ramp + extra)
    return result.at[0].set(1).at[POINTS - 1].set(MAXC)


def draw_element_stiffness(key, part):
    first_key, second_key = jax.random.split(jax.random.fold_in(key, 11))
    uniform_part = jax.random.uniform(first_key, (BLOCK, BLOCK, POINTS), jnp.float32, -1.0, 1.0)
    coupled = 0.5 * (uniform_part + jnp.transpose(uniform_part, (1, 0, 2))) * 0.15
    leading = jax.random.uniform(second_key, (BLOCK, POINTS), jnp.float32, 1.0, 2.0)
    identity = jnp.eye(BLOCK, dtype=jnp.float32)[:, :, None]
    return stiff_scale * (coupled * (1.0 - identity) + identity * leading[:, None, :])


def draw_stiffness_micro(key, part):
    first_key, second_key = jax.random.split(jax.random.fold_in(key, 23))
    uniform_part = jax.random.uniform(first_key, (NS, NS), jnp.float32, -1.0, 1.0)
    coupled = 0.5 * (uniform_part + uniform_part.T) * (0.9 / (NS - 1))
    leading = jax.random.uniform(second_key, (NS,), jnp.float32, 1.0, 2.0)
    identity = jnp.eye(NS, dtype=jnp.float32)
    return coupled * (1.0 - identity) + identity * leading[None, :]


def draw_tangent_inverse(key, part):
    first_key, second_key = jax.random.split(jax.random.fold_in(key, 37))
    spread = jax.random.uniform(first_key, (NS, NS), jnp.float32, -1.0, 1.0) * (0.1 / (NS - 1))
    leading = jax.random.uniform(second_key, (NS,), jnp.float32, 0.04, 0.08)
    identity = jnp.eye(NS, dtype=jnp.float32)
    return spread * (1.0 - identity) + identity * leading[None, :]


def block_levels(own_key, dims, shards, least, high):
    gain = 1.0
    for position, parts in shards:
        draws = jax.random.uniform(jax.random.fold_in(jax.random.fold_in(own_key, 6), position), (parts,), jnp.float32, least / len(shards), high / len(shards))
        gain = gain * jnp.repeat(jnp.exp(draws), dims[position] // parts).reshape((-1,) + (1,) * (len(dims) - 1 - position))
    return gain


def bell_draw(rng, shape, width, most, cuts=(), kind=jnp.bfloat16):
    factor_of = block_levels(rng, shape, cuts, -0.22, 0.18) if cuts else 1.0
    drawn = jax.random.normal(rng, shape, jnp.float32) * width * factor_of
    return jnp.minimum(jnp.maximum(drawn, -most), most).astype(kind)


def setup_inputs(seed: int = 0, part: int = 0) -> dict:
    arg_keys = jax.random.split(jax.random.key(seed), 12)
    part_splits = jax.random.split(jax.random.fold_in(arg_keys[11], part), 12)
    slip_state = bell_draw(part_splits[0], (POINTS, NS), 1.0, 6.0, ((0, 16),), jnp.float32)
    strain = bell_draw(part_splits[1], (BLOCK, POINTS), 1.0, 6.0, ((1, 16),), jnp.float32)
    counts = draw_counts(jax.random.fold_in(jax.random.fold_in(arg_keys[11], part), 71), part)
    element_stiffness = draw_element_stiffness(jax.random.fold_in(jax.random.fold_in(arg_keys[11], part), 71), part)
    foundation = jnp.clip(jnp.exp(math.log(0.1) - 2.3025851 * jax.random.uniform(part_splits[4], (BLOCK, POINTS), jnp.float32) ** block_levels(part_splits[4], (BLOCK, POINTS), ((1, 16),), -0.2, 0.2)), 0.01, 0.1)
    external_load = bell_draw(part_splits[5], (BLOCK, POINTS), 1.0, 6.0, ((1, 16),), jnp.float32)
    stiffness_micro = draw_stiffness_micro(jax.random.fold_in(arg_keys[11], 71), part)
    tangent_inverse = draw_tangent_inverse(jax.random.fold_in(arg_keys[11], 71), part)
    friction_limit = jnp.clip(jnp.exp(jax.random.uniform(arg_keys[8], (NS,), jnp.float32, math.log(0.2), math.log(2.0))), 0.2, 2.0)
    slip_scale = jnp.clip(jnp.exp(jax.random.uniform(arg_keys[9], (NS,), jnp.float32, math.log(0.3), math.log(3.0))), 0.3, 3.0)
    section_map = bell_draw(arg_keys[10], (BLOCK, NS), BLOCK ** -0.5, 2.5, (), jnp.float32)
    return dict(slip_state=slip_state, strain=strain, counts=counts, element_stiffness=element_stiffness, foundation=foundation, external_load=external_load, stiffness_micro=stiffness_micro, tangent_inverse=tangent_inverse, friction_limit=friction_limit, slip_scale=slip_scale, section_map=section_map)


highest = lax.Precision.HIGHEST

def relax_points(states, loads, steps_left, stiffness_micro, tangent_inverse, friction_limit, slip_scale):
    for newton in range(NEWTON):
        weight = (newton + 1.0) / NEWTON

        def sweep(sweep_index, current):
            residual = jnp.dot(current, stiffness_micro, precision=highest) + friction_limit * jnp.tanh(current / slip_scale) - weight * loads
            moved = current - jnp.dot(residual, tangent_inverse, precision=highest)
            return jnp.where(sweep_index < steps_left[:, None], moved, current)
        states = lax.fori_loop(0, MAXC, sweep, states)
    return states

def reference(slip_state, strain, counts, element_stiffness, foundation, external_load, stiffness_micro, tangent_inverse, friction_limit, slip_scale, section_map):
    loads = jnp.dot(strain.T, section_map, precision=highest)
    new_slip = relax_points(slip_state, loads, counts, stiffness_micro, tangent_inverse, friction_limit, slip_scale)
    stress = jnp.dot(section_map, new_slip.T, precision=highest) / math.sqrt(NS)
    forcing = (external_load - stress).T
    element_rows = jnp.moveaxis(element_stiffness, 2, 0)
    before = jnp.concatenate([jnp.zeros((1, BLOCK, BLOCK), jnp.float32), element_rows[:-1]], 0)
    identity = jnp.eye(BLOCK, dtype=jnp.float32)
    diagonal = before + element_rows + identity[None] * foundation.T[:, None, :]

    def forward(carry, pieces):
        inverse_prev, solved_prev = carry
        couple, block, source = pieces
        schur = block - jnp.dot(couple, jnp.dot(inverse_prev, couple, precision=highest), precision=highest)
        total = source + jnp.dot(couple, solved_prev, precision=highest)
        inverse_now = jnp.linalg.solve(schur, identity)
        solved_now = jnp.dot(inverse_now, total, precision=highest)
        return ((inverse_now, solved_now), (inverse_now, solved_now))
    start = (jnp.zeros((BLOCK, BLOCK), jnp.float32), jnp.zeros((BLOCK,), jnp.float32))
    final_carry, (inverses, partial_values) = lax.scan(forward, start, (before, diagonal, forcing))

    def backward(after_value, pieces):
        inverse_now, solved_now, couple = pieces
        value = solved_now + jnp.dot(inverse_now, jnp.dot(couple, after_value, precision=highest), precision=highest)
        return (value, value)
    last_value, values = lax.scan(backward, jnp.zeros((BLOCK,), jnp.float32), (inverses, partial_values, element_rows), reverse=True)
    return (new_slip, values.T)
```

```python
import functools
import math

import jax
import jax.numpy as jnp
from jax import lax
from jax.experimental import pallas as pl
from jax.experimental.pallas import tpu as pltpu
from jax.sharding import PartitionSpec as P

NEWTON = 2
MAXC = 12
SUB = 8
LANES = 128
ROPE = ("arc", "sec", "rep")
MESH = pl.DeviceIdType.MESH
highest = lax.Precision.HIGHEST


def split(values):
    high = values.astype(jnp.bfloat16)
    low = (values - high.astype(jnp.float32)).astype(jnp.bfloat16)
    return high, low


def bdot(left, right):
    return jnp.dot(left, right, preferred_element_type=jnp.float32)


def block_product(left, right):
    total = left[:, 0:1, :] * right[0:1]
    for k in range(1, left.shape[0]):
        total = total + left[:, k : k + 1, :] * right[k : k + 1]
    return total


def block_solve(matrix, parts):
    size = matrix.shape[0]
    for pivot in range(size):
        scale = 1.0 / matrix[pivot : pivot + 1, pivot : pivot + 1, :]
        factor = matrix[:, pivot : pivot + 1, :]

        def eliminated(values):
            row = values[pivot : pivot + 1] * scale
            rest = values - factor * row
            rows = [rest[:pivot]] * (pivot > 0) + [row] + [rest[pivot + 1 :]] * (pivot < size - 1)
            return jnp.concatenate(rows, 0)

        parts = [eliminated(values) for values in parts]
        if pivot < size - 1:
            matrix = eliminated(matrix)
    return parts


def doubling(state, steps, least, most):
    size, _, lanes = state[0].shape
    shape = (size, SUB, lanes)
    lane = lax.broadcasted_iota(jnp.int32, shape, 2)
    identity = jnp.where(
        lax.broadcasted_iota(jnp.int32, shape, 0) == lax.broadcasted_iota(jnp.int32, shape, 1),
        1.0,
        0.0,
    )

    def level(_, carry):
        s, lower, upper, rest = carry
        a, b, e = block_solve(lower + upper + rest, carry[1:])
        no_left = lane < least + s
        no_right = lane >= most - s

        def rolled(values, shift):
            return pltpu.roll(values.reshape(size * SUB, lanes), shift, 1).reshape(shape)

        a_left = jnp.where(no_left, identity, rolled(a, s))
        e_left = jnp.where(no_left, 0.0, rolled(e, s))
        b_right = jnp.where(no_right, identity, rolled(b, lanes - s))
        e_right = jnp.where(no_right, 0.0, rolled(e, lanes - s))
        rest = rest + block_product(lower, e_left) + block_product(upper, e_right)
        return s * 2, block_product(lower, a_left), block_product(upper, b_right), rest

    _, lower, upper, rest = lax.fori_loop(0, steps, level, (jnp.int32(1), *state))
    return block_solve(lower + upper + rest, [lower, upper, rest])


def kernel(
    sizes,
    slip_ref,
    strain_ref,
    counts_ref,
    element_ref,
    foundation_ref,
    load_ref,
    micro_ref,
    tangent_ref,
    limit_ref,
    scale_ref,
    map_ref,
    slip_out,
    increment_out,
    weights,
    sent,
    held,
    send_sem,
    recv_sem,
):
    group = lax.axis_index("groups")
    arc_count, sec_count, rep_count = sizes
    total = arc_count * sec_count * rep_count
    me = (
        lax.axis_index("arc") * sec_count + lax.axis_index("sec")
    ) * rep_count + lax.axis_index("rep")

    def place(index):
        return (
            group,
            index // (sec_count * rep_count),
            index // rep_count % sec_count,
            index % rep_count,
        )

    barrier = pltpu.get_barrier_semaphore()

    def greet(step, carry):
        pl.semaphore_signal(
            barrier, inc=1, device_id=place((me + step) % total), device_id_type=MESH
        )
        return carry

    lax.fori_loop(1, total, greet, 0)

    points, slips = slip_ref.shape
    size = strain_ref.shape[0]

    tangent = tangent_ref[...]
    product = jnp.dot(micro_ref[...], tangent, precision=highest, preferred_element_type=jnp.float32)
    product_high, product_low = split(product)
    tangent_high, tangent_low = split(tangent)
    weights[0 * slips : 1 * slips, :] = product_high
    weights[1 * slips : 2 * slips, :] = product_high
    weights[2 * slips : 3 * slips, :] = product_low
    weights[3 * slips : 4 * slips, :] = tangent_high
    weights[4 * slips : 5 * slips, :] = tangent_high
    weights[5 * slips : 6 * slips, :] = tangent_low
    section = map_ref[...]
    section_tangent = jnp.dot(
        section, tangent, precision=highest, preferred_element_type=jnp.float32
    )
    moved_loads = lax.dot_general(
        strain_ref[...],
        section_tangent,
        (((0,), (0,)), ((), ())),
        precision=highest,
        preferred_element_type=jnp.float32,
    )
    sweeps = jnp.broadcast_to(counts_ref[...], (LANES, points)).T
    sweeps = jnp.concatenate([sweeps] * (slips // LANES), 1)
    limit = jnp.broadcast_to(limit_ref[...], (SUB, slips))[:1]
    inverse_scale = 1.0 / scale_ref[...]
    slip = slip_ref[...]
    for newton in range(NEWTON):
        weighted = moved_loads * ((newton + 1.0) / NEWTON)

        def sweep(step, values):
            friction = limit * jnp.tanh(values * inverse_scale)
            value_high, value_low = split(values)
            friction_high, friction_low = split(friction)
            left = jnp.concatenate(
                [value_high, value_low, value_high, friction_high, friction_low, friction_high], 1
            )
            change = weighted - bdot(left, weights[...])
            return jnp.where(step.astype(jnp.float32) < sweeps, values + change, values)

        slip = lax.fori_loop(0, MAXC, sweep, slip)
    slip_out[...] = slip

    stress = lax.dot_general(
        section,
        slip,
        (((1,), (1,)), ((), ())),
        precision=highest,
        preferred_element_type=jnp.float32,
    ) * (1.0 / math.sqrt(slips))
    forcing = load_ref[...] - stress

    element = jnp.concatenate(
        [element_ref[...], jnp.zeros((size, SUB - size, points), jnp.float32)], 1
    )
    shape = (size, SUB, points)
    row = lax.broadcasted_iota(jnp.int32, shape, 0)
    column = lax.broadcasted_iota(jnp.int32, shape, 1)
    lane = lax.broadcasted_iota(jnp.int32, shape, 2)

    def rolled(values, shift):
        lanes = values.shape[2]
        return pltpu.roll(values.reshape(size * SUB, lanes), shift, 1).reshape(values.shape)

    before = jnp.where(lane == 0, 0.0, rolled(element, 1))
    foundation = jnp.concatenate(
        [foundation_ref[i : i + 1, :][None] for i in range(size)], 0
    )
    forces = jnp.concatenate([forcing[i : i + 1, :][None] for i in range(size)], 0)
    support = jnp.where(row == column, foundation, 0.0) + jnp.where(column == size, forces, 0.0)
    levels = math.ceil(math.log2(points))
    a, b, e = doubling((before, element, support), levels, 1, points)

    first = jnp.concatenate(
        [
            block_product(element, rolled(b, points - 1)),
            support + block_product(element, rolled(e, points - 1)),
        ],
        0,
    ).reshape(2 * size * SUB, points)
    last = jnp.concatenate([block_product(element, a), block_product(element, e)], 0).reshape(
        2 * size * SUB, points
    )
    fill = jnp.zeros((LANES - 2 * size * SUB, points), jnp.float32)
    first = jnp.concatenate([first, fill], 0).T[0:1]
    last = jnp.concatenate([last, fill], 0).T[points - 1 : points]
    packed = jnp.concatenate([first, last], 0)
    sent[...] = packed
    held[me] = packed
    pl.semaphore_wait(barrier, total - 1)

    def copy(step, slot, peer):
        return pltpu.make_async_remote_copy(
            src_ref=sent,
            dst_ref=held.at[slot],
            send_sem=send_sem.at[step],
            recv_sem=recv_sem.at[slot],
            device_id=place(peer),
            device_id_type=MESH,
        )

    def send(step, carry):
        copy(step, me, (me + step) % total).start()
        return carry

    lax.fori_loop(1, total, send, 0)

    def receive(step, carry):
        peer = (me + step) % total
        copy(step, peer, peer).wait_recv()
        return carry

    lax.fori_loop(1, total, receive, 0)

    wide = -(-total // LANES) * LANES

    def columns(values):
        if wide > total:
            values = jnp.concatenate([values, jnp.zeros((wide - total, LANES), jnp.float32)], 0)
        turned = [values[k : k + LANES].T for k in range(0, wide, LANES)]
        turned = turned[0] if len(turned) == 1 else jnp.concatenate(turned, 1)
        return turned[: 2 * size * SUB].reshape(2, size, SUB, wide)

    own = columns(held[:, 0, :])
    other = columns(held[:, 1, :])
    lane = lax.broadcasted_iota(jnp.int32, (size, SUB, wide), 2)
    from_left = jnp.where(lane == 0, 0.0, rolled(other[0], 1))
    support = own[1] + jnp.where(lane == 0, 0.0, rolled(other[1], 1))
    state = (from_left, own[0], support)
    faces = doubling(state, math.ceil(math.log2(total)), 0, total)[2][:, size, :]
    lane = lax.broadcasted_iota(jnp.int32, (size, wide), 1)

    def face(index):
        chosen = jnp.where((lane == index) & (lane < total), faces, 0.0)
        return jnp.sum(chosen, axis=1, keepdims=True)

    def padded(values):
        return jnp.concatenate([values, jnp.zeros((SUB - size, 1), jnp.float32)], 0)[None]

    own_face, next_face = face(me), face(me + 1)
    increment = e[:, size, :] + jnp.sum(a * padded(own_face) + b * padded(next_face), axis=1)
    lane = lax.broadcasted_iota(jnp.int32, (size, points), 1)
    increment_out[...] = jnp.where(lane == 0, own_face, increment)

    def sent_all(step, carry):
        copy(step, me, (me + step) % total).wait_send()
        return carry

    lax.fori_loop(1, total, sent_all, 0)


def solution(mesh):
    sizes = tuple(mesh.shape[axis] for axis in ROPE)
    total = math.prod(sizes)
    nodes = P(("groups",) + ROPE)
    along = P(None, ("groups",) + ROPE)

    def shards(slip, strain, counts, element, foundation, load, micro, tangent, limit, scale, section):
        slips = slip.shape[1]
        vmem = pl.BlockSpec(memory_space=pltpu.VMEM)
        return pl.pallas_call(
            functools.partial(kernel, sizes),
            out_shape=(
                jax.ShapeDtypeStruct(slip.shape, jnp.float32),
                jax.ShapeDtypeStruct(strain.shape, jnp.float32),
            ),
            in_specs=[vmem] * 11,
            out_specs=(vmem, vmem),
            scratch_shapes=[
                pltpu.VMEM((6 * slips, slips), jnp.bfloat16),
                pltpu.VMEM((2, LANES), jnp.float32),
                pltpu.VMEM((total, 2, LANES), jnp.float32),
                pltpu.SemaphoreType.DMA((total,)),
                pltpu.SemaphoreType.DMA((total,)),
            ],
            compiler_params=pltpu.CompilerParams(
                collective_id=0, has_side_effects=True, vmem_limit_bytes=32 << 20
            ),
            name="rope",
        )(
            slip,
            strain,
            counts.astype(jnp.float32).reshape(1, -1),
            element,
            foundation,
            load,
            micro,
            tangent,
            limit.reshape(1, -1),
            scale.reshape(1, -1),
            section,
        )

    return jax.shard_map(
        shards,
        mesh=mesh,
        in_specs=(
            P(("groups",) + ROPE, None),
            along,
            nodes,
            P(None, None, ("groups",) + ROPE),
            along,
            along,
            P(),
            P(),
            P(),
            P(),
            P(),
        ),
        out_specs=(P(("groups",) + ROPE, None), along),
        check_vma=False,
    )
```

```python
import functools
import math

import jax
import jax.numpy as jnp
from jax import lax
from jax.experimental import pallas as pl
from jax.experimental.pallas import tpu as pltpu
from jax.sharding import PartitionSpec as P

NEWTON = 2
MAXC = 12
OPERANDS = 11
ORDER = (7, 6, 10, 1, 0, 2, 8, 9, 3, 4, 5)
SUB = 8
LANES = 128
ROPE = ("arc", "sec", "rep")
MESH = pl.DeviceIdType.MESH
highest = lax.Precision.HIGHEST


def split(values):
    high = values.astype(jnp.bfloat16)
    low = (values - high.astype(jnp.float32)).astype(jnp.bfloat16)
    return high, low


def bdot(left, right):
    return jnp.dot(left, right, preferred_element_type=jnp.float32)


def block_product(left, right):
    total = left[:, 0:1, :] * right[0:1]
    for k in range(1, left.shape[0]):
        total = total + left[:, k : k + 1, :] * right[k : k + 1]
    return total


def block_solve(matrix, parts):
    size = matrix.shape[0]
    for pivot in range(size):
        scale = 1.0 / matrix[pivot : pivot + 1, pivot : pivot + 1, :]
        factor = matrix[:, pivot : pivot + 1, :]

        def eliminated(values):
            row = values[pivot : pivot + 1] * scale
            rest = values - factor * row
            rows = [rest[:pivot]] * (pivot > 0) + [row] + [rest[pivot + 1 :]] * (pivot < size - 1)
            return jnp.concatenate(rows, 0)

        parts = [eliminated(values) for values in parts]
        if pivot < size - 1:
            matrix = eliminated(matrix)
    return parts


def doubling(state, steps, least, most):
    size, _, lanes = state[0].shape
    shape = (size, SUB, lanes)
    lane = lax.broadcasted_iota(jnp.int32, shape, 2)
    identity = jnp.where(
        lax.broadcasted_iota(jnp.int32, shape, 0) == lax.broadcasted_iota(jnp.int32, shape, 1),
        1.0,
        0.0,
    )

    def level(_, carry):
        s, lower, upper, rest = carry
        a, b, e = block_solve(lower + upper + rest, carry[1:])
        no_left = lane < least + s
        no_right = lane >= most - s

        def rolled(values, shift):
            return pltpu.roll(values.reshape(size * SUB, lanes), shift, 1).reshape(shape)

        a_left = jnp.where(no_left, identity, rolled(a, s))
        e_left = jnp.where(no_left, 0.0, rolled(e, s))
        b_right = jnp.where(no_right, identity, rolled(b, lanes - s))
        e_right = jnp.where(no_right, 0.0, rolled(e, lanes - s))
        rest = rest + block_product(lower, e_left) + block_product(upper, e_right)
        return s * 2, block_product(lower, a_left), block_product(upper, b_right), rest

    _, lower, upper, rest = lax.fori_loop(0, steps, level, (jnp.int32(1), *state))
    return block_solve(lower + upper + rest, [lower, upper, rest])


def kernel(sizes, *refs):
    given, (slip_out, increment_out), rest = refs[:OPERANDS], refs[OPERANDS : OPERANDS + 2], refs[OPERANDS + 2 :]
    local, (weights, held, load_sem, send_sem, recv_sem) = rest[:OPERANDS], rest[OPERANDS:]
    copies = [
        pltpu.make_async_copy(source, target, load_sem.at[k])
        for k, (source, target) in enumerate(zip(given, local))
    ]
    for k in ORDER:
        copies[k].start()
    (
        slip_ref,
        strain_ref,
        counts_ref,
        element_ref,
        foundation_ref,
        load_ref,
        micro_ref,
        tangent_ref,
        limit_ref,
        scale_ref,
        map_ref,
    ) = local
    group = lax.axis_index("groups")
    arc_count, sec_count, rep_count = sizes
    total = arc_count * sec_count * rep_count
    me = (
        lax.axis_index("arc") * sec_count + lax.axis_index("sec")
    ) * rep_count + lax.axis_index("rep")

    def place(index):
        return (
            group,
            index // (sec_count * rep_count),
            index // rep_count % sec_count,
            index % rep_count,
        )

    barrier = pltpu.get_barrier_semaphore()

    def peer(step):
        return (me + step) % total

    def each(act):
        if total <= 16:
            for step in range(1, total):
                act(step)
        else:
            pl.loop(1, total)(act)

    each(
        lambda step: pl.semaphore_signal(
            barrier, inc=1, device_id=place(peer(step)), device_id_type=MESH
        )
    )

    points, slips = slip_ref.shape
    size = strain_ref.shape[0]
    for k in ORDER:
        copies[k].wait()

    tangent = tangent_ref[...]
    product = jnp.dot(micro_ref[...], tangent, precision=highest, preferred_element_type=jnp.float32)
    product_high, product_low = split(product)
    tangent_high, tangent_low = split(tangent)
    weights[0 * slips : 1 * slips, :] = product_high
    weights[1 * slips : 2 * slips, :] = product_high
    weights[2 * slips : 3 * slips, :] = product_low
    weights[3 * slips : 4 * slips, :] = tangent_high
    weights[4 * slips : 5 * slips, :] = tangent_high
    weights[5 * slips : 6 * slips, :] = tangent_low
    section = map_ref[...]
    section_tangent = jnp.dot(
        section, tangent, precision=highest, preferred_element_type=jnp.float32
    )
    moved_loads = lax.dot_general(
        strain_ref[...],
        section_tangent,
        (((0,), (0,)), ((), ())),
        precision=highest,
        preferred_element_type=jnp.float32,
    )
    sweeps = jnp.broadcast_to(counts_ref[...].astype(jnp.float32), (LANES, points)).T
    sweeps = jnp.concatenate([sweeps] * (slips // LANES), 1)
    limit = jnp.broadcast_to(limit_ref[...], (SUB, slips))[:1]
    inverse_scale = 1.0 / scale_ref[...]
    slip = slip_ref[...]
    for newton in range(NEWTON):
        weighted = moved_loads * ((newton + 1.0) / NEWTON)

        def sweep(step, values):
            friction = limit * jnp.tanh(values * inverse_scale)
            value_high, value_low = split(values)
            friction_high, friction_low = split(friction)
            left = jnp.concatenate(
                [value_high, value_low, value_high, friction_high, friction_low, friction_high], 1
            )
            change = weighted - bdot(left, weights[...])
            return jnp.where(step.astype(jnp.float32) < sweeps, values + change, values)

        slip = lax.fori_loop(0, MAXC, sweep, slip)
    slip_out[...] = slip

    stress = lax.dot_general(
        section,
        slip,
        (((1,), (1,)), ((), ())),
        precision=highest,
        preferred_element_type=jnp.float32,
    ) * (1.0 / math.sqrt(slips))
    forcing = load_ref[...] - stress

    element = jnp.concatenate(
        [element_ref[...], jnp.zeros((size, SUB - size, points), jnp.float32)], 1
    )
    shape = (size, SUB, points)
    row = lax.broadcasted_iota(jnp.int32, shape, 0)
    column = lax.broadcasted_iota(jnp.int32, shape, 1)
    lane = lax.broadcasted_iota(jnp.int32, shape, 2)

    def rolled(values, shift):
        lanes = values.shape[2]
        return pltpu.roll(values.reshape(size * SUB, lanes), shift, 1).reshape(values.shape)

    before = jnp.where(lane == 0, 0.0, rolled(element, 1))
    foundation = jnp.concatenate(
        [foundation_ref[i : i + 1, :][None] for i in range(size)], 0
    )
    forces = jnp.concatenate([forcing[i : i + 1, :][None] for i in range(size)], 0)
    support = jnp.where(row == column, foundation, 0.0) + jnp.where(column == size, forces, 0.0)
    levels = math.ceil(math.log2(points))
    a, b, e = doubling((before, element, support), levels, 1, points)

    first = jnp.concatenate(
        [
            block_product(element, rolled(b, points - 1)),
            support + block_product(element, rolled(e, points - 1)),
        ],
        0,
    ).reshape(2 * size * SUB, points)
    last = jnp.concatenate([block_product(element, a), block_product(element, e)], 0).reshape(
        2 * size * SUB, points
    )
    fill = jnp.zeros((LANES - 2 * size * SUB, points), jnp.float32)
    first = jnp.concatenate([first, fill], 0).T[0:1]
    last = jnp.concatenate([last, fill], 0).T[points - 1 : points]
    packed = jnp.concatenate([first, last], 0)
    held[me] = packed
    pl.semaphore_wait(barrier, total - 1)

    def copy(step, slot):
        return pltpu.make_async_remote_copy(
            src_ref=held.at[slot],
            dst_ref=held.at[slot],
            send_sem=send_sem.at[step],
            recv_sem=recv_sem.at[slot],
            device_id=place(peer(step)),
            device_id_type=MESH,
        )

    each(lambda step: copy(step, me).start())
    each(lambda step: copy(step, peer(step)).wait_recv())

    wide = -(-total // LANES) * LANES

    def columns(values):
        if wide > total:
            values = jnp.concatenate([values, jnp.zeros((wide - total, LANES), jnp.float32)], 0)
        turned = [values[k : k + LANES].T for k in range(0, wide, LANES)]
        turned = turned[0] if len(turned) == 1 else jnp.concatenate(turned, 1)
        return turned[: 2 * size * SUB].reshape(2, size, SUB, wide)

    own = columns(held[:, 0, :])
    other = columns(held[:, 1, :])
    lane = lax.broadcasted_iota(jnp.int32, (size, SUB, wide), 2)
    from_left = jnp.where(lane == 0, 0.0, rolled(other[0], 1))
    support = own[1] + jnp.where(lane == 0, 0.0, rolled(other[1], 1))
    state = (from_left, own[0], support)
    faces = doubling(state, math.ceil(math.log2(total)), 0, total)[2][:, size, :]
    lane = lax.broadcasted_iota(jnp.int32, (size, wide), 1)

    def face(index):
        chosen = jnp.where((lane == index) & (lane < total), faces, 0.0)
        return jnp.sum(chosen, axis=1, keepdims=True)

    def padded(values):
        return jnp.concatenate([values, jnp.zeros((SUB - size, 1), jnp.float32)], 0)[None]

    own_face, next_face = face(me), face(me + 1)
    increment = e[:, size, :] + jnp.sum(a * padded(own_face) + b * padded(next_face), axis=1)
    lane = lax.broadcasted_iota(jnp.int32, (size, points), 1)
    increment_out[...] = jnp.where(lane == 0, own_face, increment)

    each(lambda step: copy(step, me).wait_send())


def solution(mesh):
    sizes = tuple(mesh.shape[axis] for axis in ROPE)
    total = math.prod(sizes)
    nodes = P(("groups",) + ROPE)
    along = P(None, ("groups",) + ROPE)

    def shards(slip, strain, counts, element, foundation, load, micro, tangent, limit, scale, section):
        slips = slip.shape[1]
        operands = (
            slip,
            strain,
            counts.reshape(1, -1),
            element,
            foundation,
            load,
            micro,
            tangent,
            limit.reshape(1, -1),
            scale.reshape(1, -1),
            section,
        )
        vmem = pl.BlockSpec(memory_space=pltpu.VMEM)
        return pl.pallas_call(
            functools.partial(kernel, sizes),
            out_shape=(
                jax.ShapeDtypeStruct(slip.shape, jnp.float32),
                jax.ShapeDtypeStruct(strain.shape, jnp.float32),
            ),
            in_specs=[pl.BlockSpec(memory_space=pltpu.HBM)] * OPERANDS,
            out_specs=(vmem, vmem),
            scratch_shapes=[pltpu.VMEM(value.shape, value.dtype) for value in operands]
            + [
                pltpu.VMEM((6 * slips, slips), jnp.bfloat16),
                pltpu.VMEM((total, 2, LANES), jnp.float32),
                pltpu.SemaphoreType.DMA((OPERANDS,)),
                pltpu.SemaphoreType.DMA((total,)),
                pltpu.SemaphoreType.DMA((total,)),
            ],
            compiler_params=pltpu.CompilerParams(
                collective_id=0, has_side_effects=True, vmem_limit_bytes=32 << 20
            ),
            name="rope",
        )(*[pltpu.with_memory_space_constraint(value, pltpu.HBM) for value in operands])

    return jax.shard_map(
        shards,
        mesh=mesh,
        in_specs=(
            P(("groups",) + ROPE, None),
            along,
            nodes,
            P(None, None, ("groups",) + ROPE),
            along,
            along,
            P(),
            P(),
            P(),
            P(),
            P(),
        ),
        out_specs=(P(("groups",) + ROPE, None), along),
        check_vma=False,
    )
```

```python
import functools
import math

import jax
import jax.numpy as jnp
from jax import lax
from jax.experimental import pallas as pl
from jax.experimental.pallas import tpu as pltpu
from jax.sharding import PartitionSpec as P

NEWTON = 2
MAXC = 12
OPERANDS = 11
ORDER = (7, 6, 10, 1, 0, 2, 8, 9, 3, 4, 5)
SUB = 8
LANES = 128
ROPE = ("arc", "sec", "rep")
MESH = pl.DeviceIdType.MESH
highest = lax.Precision.HIGHEST


def split(values):
    high = values.astype(jnp.bfloat16)
    low = (values - high.astype(jnp.float32)).astype(jnp.bfloat16)
    return high, low


def bdot(left, right):
    return jnp.dot(left, right, preferred_element_type=jnp.float32)


def block_product(left, right):
    total = left[:, 0:1, :] * right[0:1]
    for k in range(1, left.shape[0]):
        total = total + left[:, k : k + 1, :] * right[k : k + 1]
    return total


def block_solve(matrix, parts):
    size = matrix.shape[0]
    for pivot in range(size):
        scale = 1.0 / matrix[pivot : pivot + 1, pivot : pivot + 1, :]
        factor = matrix[:, pivot : pivot + 1, :]

        def eliminated(values):
            row = values[pivot : pivot + 1] * scale
            rest = values - factor * row
            rows = [rest[:pivot]] * (pivot > 0) + [row] + [rest[pivot + 1 :]] * (pivot < size - 1)
            return jnp.concatenate(rows, 0)

        parts = [eliminated(values) for values in parts]
        if pivot < size - 1:
            matrix = eliminated(matrix)
    return parts


def doubling(state, steps, least, most, beside=None, others=()):
    size, _, lanes = state[0].shape
    shape = (size, SUB, lanes)
    lane = lax.broadcasted_iota(jnp.int32, shape, 2)
    identity = jnp.where(
        lax.broadcasted_iota(jnp.int32, shape, 0) == lax.broadcasted_iota(jnp.int32, shape, 1),
        1.0,
        0.0,
    )

    def level(step, carry):
        s, lower, upper, rest, *others = carry
        a, b, e = block_solve(lower + upper + rest, [lower, upper, rest])
        if beside is not None:
            others = [beside(step, *others)]
        no_left = lane < least + s
        no_right = lane >= most - s

        def rolled(values, shift):
            return pltpu.roll(values.reshape(size * SUB, lanes), shift, 1).reshape(shape)

        a_left = jnp.where(no_left, identity, rolled(a, s))
        e_left = jnp.where(no_left, 0.0, rolled(e, s))
        b_right = jnp.where(no_right, identity, rolled(b, lanes - s))
        e_right = jnp.where(no_right, 0.0, rolled(e, lanes - s))
        rest = rest + block_product(lower, e_left) + block_product(upper, e_right)
        return s * 2, block_product(lower, a_left), block_product(upper, b_right), rest, *others

    _, lower, upper, rest, *others = lax.fori_loop(
        0, steps, level, (jnp.int32(1), *state, *others)
    )
    return (*block_solve(lower + upper + rest, [lower, upper, rest]), *others)


def kernel(sizes, *refs):
    given, (slip_out, increment_out), rest = refs[:OPERANDS], refs[OPERANDS : OPERANDS + 2], refs[OPERANDS + 2 :]
    local, (weights, held, load_sem, send_sem, recv_sem) = rest[:OPERANDS], rest[OPERANDS:]
    copies = [
        pltpu.make_async_copy(source, target, load_sem.at[k])
        for k, (source, target) in enumerate(zip(given, local))
    ]
    for k in ORDER:
        copies[k].start()
    (
        slip_ref,
        strain_ref,
        counts_ref,
        element_ref,
        foundation_ref,
        load_ref,
        micro_ref,
        tangent_ref,
        limit_ref,
        scale_ref,
        map_ref,
    ) = local
    group = lax.axis_index("groups")
    arc_count, sec_count, rep_count = sizes
    total = arc_count * sec_count * rep_count
    me = (
        lax.axis_index("arc") * sec_count + lax.axis_index("sec")
    ) * rep_count + lax.axis_index("rep")

    def place(index):
        return (
            group,
            index // (sec_count * rep_count),
            index // rep_count % sec_count,
            index % rep_count,
        )

    barrier = pltpu.get_barrier_semaphore()

    def peer(step):
        return (me + step) % total

    def each(act):
        if total <= 16:
            for step in range(1, total):
                act(step)
        else:
            pl.loop(1, total)(act)

    each(
        lambda step: pl.semaphore_signal(
            barrier, inc=1, device_id=place(peer(step)), device_id_type=MESH
        )
    )

    points, slips = slip_ref.shape
    size = strain_ref.shape[0]
    for k in ORDER:
        copies[k].wait()

    tangent = tangent_ref[...]
    product = jnp.dot(micro_ref[...], tangent, precision=highest, preferred_element_type=jnp.float32)
    product_high, product_low = split(product)
    tangent_high, tangent_low = split(tangent)
    weights[0 * slips : 1 * slips, :] = product_high
    weights[1 * slips : 2 * slips, :] = product_high
    weights[2 * slips : 3 * slips, :] = product_low
    weights[3 * slips : 4 * slips, :] = tangent_high
    weights[4 * slips : 5 * slips, :] = tangent_high
    weights[5 * slips : 6 * slips, :] = tangent_low
    section = map_ref[...]
    section_tangent = jnp.dot(
        section, tangent, precision=highest, preferred_element_type=jnp.float32
    )
    moved_loads = lax.dot_general(
        strain_ref[...],
        section_tangent,
        (((0,), (0,)), ((), ())),
        precision=highest,
        preferred_element_type=jnp.float32,
    )
    sweeps = jnp.broadcast_to(counts_ref[...].astype(jnp.float32), (LANES, points)).T
    sweeps = jnp.concatenate([sweeps] * (slips // LANES), 1)
    limit = jnp.broadcast_to(limit_ref[...], (SUB, slips))[:1]
    inverse_scale = 1.0 / scale_ref[...]
    slip = slip_ref[...]
    element = jnp.concatenate(
        [element_ref[...], jnp.zeros((size, SUB - size, points), jnp.float32)], 1
    )
    shape = (size, SUB, points)
    row = lax.broadcasted_iota(jnp.int32, shape, 0)
    column = lax.broadcasted_iota(jnp.int32, shape, 1)
    lane = lax.broadcasted_iota(jnp.int32, shape, 2)

    def rolled(values, shift):
        lanes = values.shape[2]
        return pltpu.roll(values.reshape(size * SUB, lanes), shift, 1).reshape(values.shape)

    before = jnp.where(lane == 0, 0.0, rolled(element, 1))
    foundation = jnp.concatenate(
        [foundation_ref[i : i + 1, :][None] for i in range(size)], 0
    )
    support = jnp.where(row == column, foundation, 0.0)
    levels = math.ceil(math.log2(points))

    for newton in range(NEWTON):
        weighted = moved_loads * ((newton + 1.0) / NEWTON)

        def sweep(step, values):
            friction = limit * jnp.tanh(values * inverse_scale)
            value_high, value_low = split(values)
            friction_high, friction_low = split(friction)
            left = jnp.concatenate(
                [value_high, value_low, value_high, friction_high, friction_low, friction_high], 1
            )
            change = weighted - bdot(left, weights[...])
            return jnp.where(step.astype(jnp.float32) < sweeps, values + change, values)

        done = 0
        if newton == 0 and levels <= MAXC:
            done = levels
            a, b, e, slip = doubling(
                (before, element, support), levels, 1, points, sweep, (slip,)
            )
        elif newton == 0:
            a, b, e = doubling((before, element, support), levels, 1, points)
        slip = lax.fori_loop(done, MAXC, sweep, slip)
    slip_out[...] = slip

    stress = lax.dot_general(
        section,
        slip,
        (((1,), (1,)), ((), ())),
        precision=highest,
        preferred_element_type=jnp.float32,
    ) * (1.0 / math.sqrt(slips))
    forcing = load_ref[...] - stress

    forces = jnp.concatenate([forcing[i : i + 1, :][None] for i in range(size)], 0)
    support_loaded = support + jnp.where(column == size, forces, 0.0)

    def condensed(blocks):
        total_force = jnp.sum(
            jnp.sum(jnp.where(lane == 0, 0.0, blocks) * forces, axis=0), axis=1, keepdims=True
        )
        spread = jnp.broadcast_to(total_force, (SUB, points))
        return jnp.concatenate([spread[k : k + 1][None] for k in range(size)], 0)

    first_force = forces + condensed(a)
    last_force = condensed(b)
    first = jnp.concatenate(
        [
            block_product(element, rolled(b, points - 1)),
            jnp.where(
                column == size,
                first_force,
                support + block_product(element, rolled(e, points - 1)),
            ),
        ],
        0,
    ).reshape(2 * size * SUB, points)
    last = jnp.concatenate(
        [
            block_product(element, a),
            jnp.where(column == size, last_force, block_product(element, e)),
        ],
        0,
    ).reshape(2 * size * SUB, points)
    fill = jnp.zeros((LANES - 2 * size * SUB, points), jnp.float32)
    first = jnp.concatenate([first, fill], 0).T[0:1]
    last = jnp.concatenate([last, fill], 0).T[points - 1 : points]
    packed = jnp.concatenate([first, last], 0)
    held[me] = packed
    pl.semaphore_wait(barrier, total - 1)

    def copy(step, slot):
        return pltpu.make_async_remote_copy(
            src_ref=held.at[slot],
            dst_ref=held.at[slot],
            send_sem=send_sem.at[step],
            recv_sem=recv_sem.at[slot],
            device_id=place(peer(step)),
            device_id_type=MESH,
        )

    each(lambda step: copy(step, me).start())
    e = doubling((before, element, support_loaded), levels, 1, points)[2]
    each(lambda step: copy(step, peer(step)).wait_recv())

    wide = -(-total // LANES) * LANES

    def columns(values):
        if wide > total:
            values = jnp.concatenate([values, jnp.zeros((wide - total, LANES), jnp.float32)], 0)
        turned = [values[k : k + LANES].T for k in range(0, wide, LANES)]
        turned = turned[0] if len(turned) == 1 else jnp.concatenate(turned, 1)
        return turned[: 2 * size * SUB].reshape(2, size, SUB, wide)

    own = columns(held[:, 0, :])
    other = columns(held[:, 1, :])
    lane = lax.broadcasted_iota(jnp.int32, (size, SUB, wide), 2)
    from_left = jnp.where(lane == 0, 0.0, rolled(other[0], 1))
    support = own[1] + jnp.where(lane == 0, 0.0, rolled(other[1], 1))
    state = (from_left, own[0], support)
    faces = doubling(state, math.ceil(math.log2(total)), 0, total)[2][:, size, :]
    lane = lax.broadcasted_iota(jnp.int32, (size, wide), 1)

    def face(index):
        chosen = jnp.where((lane == index) & (lane < total), faces, 0.0)
        return jnp.sum(chosen, axis=1, keepdims=True)

    def padded(values):
        return jnp.concatenate([values, jnp.zeros((SUB - size, 1), jnp.float32)], 0)[None]

    own_face, next_face = face(me), face(me + 1)
    increment = e[:, size, :] + jnp.sum(a * padded(own_face) + b * padded(next_face), axis=1)
    lane = lax.broadcasted_iota(jnp.int32, (size, points), 1)
    increment_out[...] = jnp.where(lane == 0, own_face, increment)

    each(lambda step: copy(step, me).wait_send())


def solution(mesh):
    sizes = tuple(mesh.shape[axis] for axis in ROPE)
    total = math.prod(sizes)
    nodes = P(("groups",) + ROPE)
    along = P(None, ("groups",) + ROPE)

    def shards(slip, strain, counts, element, foundation, load, micro, tangent, limit, scale, section):
        slips = slip.shape[1]
        operands = (
            slip,
            strain,
            counts.reshape(1, -1),
            element,
            foundation,
            load,
            micro,
            tangent,
            limit.reshape(1, -1),
            scale.reshape(1, -1),
            section,
        )
        vmem = pl.BlockSpec(memory_space=pltpu.VMEM)
        return pl.pallas_call(
            functools.partial(kernel, sizes),
            out_shape=(
                jax.ShapeDtypeStruct(slip.shape, jnp.float32),
                jax.ShapeDtypeStruct(strain.shape, jnp.float32),
            ),
            in_specs=[pl.BlockSpec(memory_space=pltpu.HBM)] * OPERANDS,
            out_specs=(vmem, vmem),
            scratch_shapes=[pltpu.VMEM(value.shape, value.dtype) for value in operands]
            + [
                pltpu.VMEM((6 * slips, slips), jnp.bfloat16),
                pltpu.VMEM((total, 2, LANES), jnp.float32),
                pltpu.SemaphoreType.DMA((OPERANDS,)),
                pltpu.SemaphoreType.DMA((total,)),
                pltpu.SemaphoreType.DMA((total,)),
            ],
            compiler_params=pltpu.CompilerParams(
                collective_id=0, has_side_effects=True, vmem_limit_bytes=32 << 20
            ),
            name="rope",
        )(*[pltpu.with_memory_space_constraint(value, pltpu.HBM) for value in operands])

    return jax.shard_map(
        shards,
        mesh=mesh,
        in_specs=(
            P(("groups",) + ROPE, None),
            along,
            nodes,
            P(None, None, ("groups",) + ROPE),
            along,
            along,
            P(),
            P(),
            P(),
            P(),
            P(),
        ),
        out_specs=(P(("groups",) + ROPE, None), along),
        check_vma=False,
    )
```

```python
import functools
import math

import jax
import jax.numpy as jnp
from jax import lax
from jax.experimental import pallas as pl
from jax.experimental.pallas import tpu as pltpu
from jax.sharding import PartitionSpec as P

NEWTON = 2
MAXC = 12
OPERANDS = 11
ORDER = (7, 6, 10, 1, 0, 2, 8, 9, 3, 4, 5)
SUB = 8
LANES = 128
ROPE = ("arc", "sec", "rep")
MESH = pl.DeviceIdType.MESH
highest = lax.Precision.HIGHEST


def split(values):
    high = values.astype(jnp.bfloat16)
    low = (values - high.astype(jnp.float32)).astype(jnp.bfloat16)
    return high, low


def bdot(left, right):
    return jnp.dot(left, right, preferred_element_type=jnp.float32)


def block_product(left, right):
    total = left[:, 0:1, :] * right[0:1]
    for k in range(1, left.shape[0]):
        total = total + left[:, k : k + 1, :] * right[k : k + 1]
    return total


def block_solve(matrix, parts):
    size = matrix.shape[0]
    for pivot in range(size):
        scale = 1.0 / matrix[pivot : pivot + 1, pivot : pivot + 1, :]
        factor = matrix[:, pivot : pivot + 1, :]

        def eliminated(values):
            row = values[pivot : pivot + 1] * scale
            rest = values - factor * row
            rows = [rest[:pivot]] * (pivot > 0) + [row] + [rest[pivot + 1 :]] * (pivot < size - 1)
            return jnp.concatenate(rows, 0)

        parts = [eliminated(values) for values in parts]
        if pivot < size - 1:
            matrix = eliminated(matrix)
    return parts


def doubling(state, steps, least, most, beside=None, others=()):
    size, _, lanes = state[0].shape
    shape = (size, SUB, lanes)
    lane = lax.broadcasted_iota(jnp.int32, shape, 2)
    identity = jnp.where(
        lax.broadcasted_iota(jnp.int32, shape, 0) == lax.broadcasted_iota(jnp.int32, shape, 1),
        1.0,
        0.0,
    )

    def level(step, carry):
        s, lower, upper, rest, *others = carry
        a, b, e = block_solve(lower + upper + rest, [lower, upper, rest])
        if beside is not None:
            others = [beside(step, *others)]
        no_left = lane < least + s
        no_right = lane >= most - s

        def rolled(values, shift):
            return pltpu.roll(values.reshape(size * SUB, lanes), shift, 1).reshape(shape)

        a_left = jnp.where(no_left, identity, rolled(a, s))
        e_left = jnp.where(no_left, 0.0, rolled(e, s))
        b_right = jnp.where(no_right, identity, rolled(b, lanes - s))
        e_right = jnp.where(no_right, 0.0, rolled(e, lanes - s))
        rest = rest + block_product(lower, e_left) + block_product(upper, e_right)
        return s * 2, block_product(lower, a_left), block_product(upper, b_right), rest, *others

    _, lower, upper, rest, *others = lax.fori_loop(
        0, steps, level, (jnp.int32(1), *state, *others)
    )
    return (*block_solve(lower + upper + rest, [lower, upper, rest]), *others)


def kernel(sizes, *refs):
    given, (slip_out, increment_out), rest = refs[:OPERANDS], refs[OPERANDS : OPERANDS + 2], refs[OPERANDS + 2 :]
    local, (weights, held, load_sem, send_sem, recv_sem) = rest[:OPERANDS], rest[OPERANDS:]
    copies = [
        pltpu.make_async_copy(source, target, load_sem.at[k])
        for k, (source, target) in enumerate(zip(given, local))
    ]
    for k in ORDER:
        copies[k].start()
    (
        slip_ref,
        strain_ref,
        counts_ref,
        element_ref,
        foundation_ref,
        load_ref,
        micro_ref,
        tangent_ref,
        limit_ref,
        scale_ref,
        map_ref,
    ) = local
    group = lax.axis_index("groups")
    arc_count, sec_count, rep_count = sizes
    total = arc_count * sec_count * rep_count
    me = (
        lax.axis_index("arc") * sec_count + lax.axis_index("sec")
    ) * rep_count + lax.axis_index("rep")

    barrier = pltpu.get_barrier_semaphore()

    def partner(step):
        return (
            lax.rem(lax.axis_index("arc") + step // (sec_count * rep_count), arc_count),
            lax.rem(lax.axis_index("sec") + step // rep_count % sec_count, sec_count),
            lax.rem(lax.axis_index("rep") + step % rep_count, rep_count),
        )

    def peer(step):
        arc, sec, rep = partner(step)
        return (arc * sec_count + sec) * rep_count + rep

    def each(act):
        if total <= 16:
            for step in range(1, total):
                act(step)
        else:
            pl.loop(1, total)(act)

    each(
        lambda step: pl.semaphore_signal(
            barrier, inc=1, device_id=(group, *partner(step)), device_id_type=MESH
        )
    )

    points, slips = slip_ref.shape
    size = strain_ref.shape[0]
    for k in ORDER:
        copies[k].wait()

    tangent = tangent_ref[...]
    product = jnp.dot(micro_ref[...], tangent, precision=highest, preferred_element_type=jnp.float32)
    product_high, product_low = split(product)
    tangent_high, tangent_low = split(tangent)
    weights[0 * slips : 1 * slips, :] = product_high
    weights[1 * slips : 2 * slips, :] = product_high
    weights[2 * slips : 3 * slips, :] = product_low
    weights[3 * slips : 4 * slips, :] = tangent_high
    weights[4 * slips : 5 * slips, :] = tangent_high
    weights[5 * slips : 6 * slips, :] = tangent_low
    section = map_ref[...]
    section_tangent = jnp.dot(
        section, tangent, precision=highest, preferred_element_type=jnp.float32
    )
    moved_loads = lax.dot_general(
        strain_ref[...],
        section_tangent,
        (((0,), (0,)), ((), ())),
        precision=highest,
        preferred_element_type=jnp.float32,
    )
    sweeps = jnp.broadcast_to(counts_ref[...].astype(jnp.float32), (LANES, points)).T
    sweeps = jnp.concatenate([sweeps] * (slips // LANES), 1)
    limit = jnp.broadcast_to(limit_ref[...], (SUB, slips))[:1]
    inverse_scale = 1.0 / scale_ref[...]
    slip = slip_ref[...]
    element = jnp.concatenate(
        [element_ref[...], jnp.zeros((size, SUB - size, points), jnp.float32)], 1
    )
    shape = (size, SUB, points)
    row = lax.broadcasted_iota(jnp.int32, shape, 0)
    column = lax.broadcasted_iota(jnp.int32, shape, 1)
    lane = lax.broadcasted_iota(jnp.int32, shape, 2)

    def rolled(values, shift):
        lanes = values.shape[2]
        return pltpu.roll(values.reshape(size * SUB, lanes), shift, 1).reshape(values.shape)

    before = jnp.where(lane == 0, 0.0, rolled(element, 1))
    foundation = jnp.concatenate(
        [foundation_ref[i : i + 1, :][None] for i in range(size)], 0
    )
    support = jnp.where(row == column, foundation, 0.0)
    levels = math.ceil(math.log2(points))

    for newton in range(NEWTON):
        weighted = moved_loads * ((newton + 1.0) / NEWTON)

        def sweep(step, values):
            friction = limit * jnp.tanh(values * inverse_scale)
            value_high, value_low = split(values)
            friction_high, friction_low = split(friction)
            left = jnp.concatenate(
                [value_high, value_low, value_high, friction_high, friction_low, friction_high], 1
            )
            change = weighted - bdot(left, weights[...])
            return jnp.where(step.astype(jnp.float32) < sweeps, values + change, values)

        done = 0
        if newton == 0 and levels <= MAXC:
            done = levels
            a, b, e, slip = doubling(
                (before, element, support), levels, 1, points, sweep, (slip,)
            )
        elif newton == 0:
            a, b, e = doubling((before, element, support), levels, 1, points)
        slip = lax.fori_loop(done, MAXC, sweep, slip)
    slip_out[...] = slip

    stress = lax.dot_general(
        section,
        slip,
        (((1,), (1,)), ((), ())),
        precision=highest,
        preferred_element_type=jnp.float32,
    ) * (1.0 / math.sqrt(slips))
    forcing = load_ref[...] - stress

    forces = jnp.concatenate([forcing[i : i + 1, :][None] for i in range(size)], 0)
    support_loaded = support + jnp.where(column == size, forces, 0.0)

    def condensed(blocks):
        total_force = jnp.sum(
            jnp.sum(jnp.where(lane == 0, 0.0, blocks) * forces, axis=0), axis=1, keepdims=True
        )
        spread = jnp.broadcast_to(total_force, (SUB, points))
        return jnp.concatenate([spread[k : k + 1][None] for k in range(size)], 0)

    first_force = forces + condensed(a)
    last_force = condensed(b)
    first = jnp.concatenate(
        [
            block_product(element, rolled(b, points - 1)),
            jnp.where(
                column == size,
                first_force,
                support + block_product(element, rolled(e, points - 1)),
            ),
        ],
        0,
    ).reshape(2 * size * SUB, points)
    last = jnp.concatenate(
        [
            block_product(element, a),
            jnp.where(column == size, last_force, block_product(element, e)),
        ],
        0,
    ).reshape(2 * size * SUB, points)
    fill = jnp.zeros((LANES - 2 * size * SUB, points), jnp.float32)
    first = jnp.concatenate([first, fill], 0).T[0:1]
    last = jnp.concatenate([last, fill], 0).T[points - 1 : points]
    packed = jnp.concatenate([first, last], 0)
    held[me] = packed
    pl.semaphore_wait(barrier, total - 1)

    def copy(step, slot):
        return pltpu.make_async_remote_copy(
            src_ref=held.at[slot],
            dst_ref=held.at[slot],
            send_sem=send_sem.at[step],
            recv_sem=recv_sem.at[slot],
            device_id=(group, *partner(step)),
            device_id_type=MESH,
        )

    each(lambda step: copy(step, me).start())
    e = doubling((before, element, support_loaded), levels, 1, points)[2]
    each(lambda step: copy(step, peer(step)).wait_recv())

    wide = -(-total // LANES) * LANES

    def columns(values):
        if wide > total:
            values = jnp.concatenate([values, jnp.zeros((wide - total, LANES), jnp.float32)], 0)
        turned = [values[k : k + LANES].T for k in range(0, wide, LANES)]
        turned = turned[0] if len(turned) == 1 else jnp.concatenate(turned, 1)
        return turned[: 2 * size * SUB].reshape(2, size, SUB, wide)

    own = columns(held[:, 0, :])
    other = columns(held[:, 1, :])
    lane = lax.broadcasted_iota(jnp.int32, (size, SUB, wide), 2)
    from_left = jnp.where(lane == 0, 0.0, rolled(other[0], 1))
    support = own[1] + jnp.where(lane == 0, 0.0, rolled(other[1], 1))
    state = (from_left, own[0], support)
    faces = doubling(state, math.ceil(math.log2(total)), 0, total)[2][:, size, :]
    lane = lax.broadcasted_iota(jnp.int32, (size, wide), 1)

    def face(index):
        chosen = jnp.where((lane == index) & (lane < total), faces, 0.0)
        return jnp.sum(chosen, axis=1, keepdims=True)

    def padded(values):
        return jnp.concatenate([values, jnp.zeros((SUB - size, 1), jnp.float32)], 0)[None]

    own_face, next_face = face(me), face(me + 1)
    increment = e[:, size, :] + jnp.sum(a * padded(own_face) + b * padded(next_face), axis=1)
    lane = lax.broadcasted_iota(jnp.int32, (size, points), 1)
    increment_out[...] = jnp.where(lane == 0, own_face, increment)

    each(lambda step: copy(step, me).wait_send())


def solution(mesh):
    sizes = tuple(mesh.shape[axis] for axis in ROPE)
    total = math.prod(sizes)
    nodes = P(("groups",) + ROPE)
    along = P(None, ("groups",) + ROPE)

    def shards(slip, strain, counts, element, foundation, load, micro, tangent, limit, scale, section):
        slips = slip.shape[1]
        operands = (
            slip,
            strain,
            counts.reshape(1, -1),
            element,
            foundation,
            load,
            micro,
            tangent,
            limit.reshape(1, -1),
            scale.reshape(1, -1),
            section,
        )
        vmem = pl.BlockSpec(memory_space=pltpu.VMEM)
        return pl.pallas_call(
            functools.partial(kernel, sizes),
            out_shape=(
                jax.ShapeDtypeStruct(slip.shape, jnp.float32),
                jax.ShapeDtypeStruct(strain.shape, jnp.float32),
            ),
            in_specs=[pl.BlockSpec(memory_space=pltpu.HBM)] * OPERANDS,
            out_specs=(vmem, vmem),
            scratch_shapes=[pltpu.VMEM(value.shape, value.dtype) for value in operands]
            + [
                pltpu.VMEM((6 * slips, slips), jnp.bfloat16),
                pltpu.VMEM((total, 2, LANES), jnp.float32),
                pltpu.SemaphoreType.DMA((OPERANDS,)),
                pltpu.SemaphoreType.DMA((total,)),
                pltpu.SemaphoreType.DMA((total,)),
            ],
            compiler_params=pltpu.CompilerParams(
                collective_id=0, has_side_effects=True, vmem_limit_bytes=32 << 20
            ),
            name="rope",
        )(*[pltpu.with_memory_space_constraint(value, pltpu.HBM) for value in operands])

    return jax.shard_map(
        shards,
        mesh=mesh,
        in_specs=(
            P(("groups",) + ROPE, None),
            along,
            nodes,
            P(None, None, ("groups",) + ROPE),
            along,
            along,
            P(),
            P(),
            P(),
            P(),
            P(),
        ),
        out_specs=(P(("groups",) + ROPE, None), along),
        check_vma=False,
    )
```
